32 devices in a mesh: row: 2 (over x), col: 8 (over z, core), pair: 2 (over y).
Axes of the slice: x: 2, y: 2, z: 4, core: 2. Of those that a mesh axis runs over, the one named last changes fastest.
Arguments:
- integrals: bfloat16 [1024, 4096], P('row', 'col'), may hold values from -0.09375 to 0.09375
- kept_tiles: int32 [64, 256], P('row', 'col'), may hold values 0 or 1
- amplitudes: bfloat16 [4096, 1536], P(('col', 'row'), 'pair'), may hold values from -6 to 6
- driver: bfloat16 [1024, 1536], P(('row', 'col', 'pair')), may hold values from -6 to 6
- vir_energy: float32 [1024], P(('row', 'col', 'pair')), may hold values from 1 to 3
- occ_energy: float32 [1536], replicated, may hold values from -1.5 to -0.25
- occ_coupling: bfloat16 [1536, 1536], replicated, may hold values from -0.15625 to 0.15625
Outputs:
- increment: float32 [1024, 1536], P(('row', 'col', 'pair'))
The draws below stay inside these ranges and needn't reach their ends.
All inputs are finite; a program needn't handle non-finite values. No bound on the sum of `kept_tiles` on one device may be relied on, other than what follows from the above.
Results may differ from the reference program's by a relative error of at most 0.0011.
Values may be sent and summed in bfloat16 or wider, within the bound.
No kernel may reach another device: no remote copies, remote signals or barrier semaphores. Data moves between devices by JAX's collectives and lax.ppermute only.
A program may use at most 64 MiB of HBM per device.

```python
import jax
import jax.numpy as jnp
from jax import lax

TILE = 16
IJ_TOTAL = 1536
PAIRS = 1024
KETS = 4096


def set_ends(result, key, least, top_value):
    extent = result.shape
    place = [jax.random.randint(jax.random.fold_in(key, axis), (), 0, extent[axis]) for axis in range(len(extent))]
    result = result.at[tuple(place)].set(least)
    longest = extent.index(max(extent))
    place[longest] = (place[longest] + 1) % extent[longest]
    return result.at[tuple(place)].set(top_value)


def levels(key, shape, split, smallest, top_value):
    gain = 1.0
    for dim, shards_of in split:
        draws = jax.random.uniform(jax.random.fold_in(jax.random.fold_in(key, 6), dim), (shards_of,), jnp.float32, smallest / len(split), top_value / len(split))
        gain = gain * jnp.repeat(jnp.exp(draws), shape[dim] // shards_of).reshape((-1,) + (1,) * (len(shape) - 1 - dim))
    return gain


def centred(rng, dims, spread, reach, pieces=(), held_as=jnp.bfloat16):
    array = spread * jax.random.normal(rng, dims, jnp.float32)
    if pieces:
        array = array * levels(rng, dims, pieces, -0.22, 0.18)
    return jnp.clip(array, -reach, reach).astype(held_as)


def setup_inputs(seed: int = 0) -> dict:
    splits = jax.random.split(jax.random.key(seed), 8)
    return {
        "integrals": centred(splits[0], (PAIRS, KETS), KETS ** -0.5, 0.09375, ((0, 2), (1, 8))),
        "kept_tiles": set_ends((jax.random.randint(splits[1], (PAIRS // TILE, KETS // TILE), 0, 4) < 3).astype(jnp.int32), jax.random.fold_in(splits[1], 1), 0, 1),
        "amplitudes": centred(splits[2], (KETS, IJ_TOTAL), 1.0, 6.0, ((0, 16), (1, 2))),
        "driver": centred(splits[3], (PAIRS, IJ_TOTAL), 1.0, 6.0, ((0, 32),)),
        "vir_energy": jnp.clip(1.0 + 2.0 * jax.random.uniform(splits[4], (PAIRS,), jnp.float32) ** levels(splits[4], (PAIRS,), ((0, 32),), -0.2, 0.2), 1.0, 3.0),
        "occ_energy": jnp.clip(jax.random.uniform(splits[5], (IJ_TOTAL,), jnp.float32, -1.5, -0.25), -1.5, -0.25),
        "occ_coupling": centred(splits[6], (IJ_TOTAL, IJ_TOTAL), IJ_TOTAL ** -0.5, 0.15625),
    }


def reference(integrals, kept_tiles, amplitudes, driver, vir_energy, occ_energy, occ_coupling):
    ampl_full = amplitudes.astype(jnp.float32)
    tile_rows = PAIRS // TILE

    def one_block(index):
        block = lax.dynamic_slice_in_dim(integrals, index * TILE, TILE, 0).astype(jnp.float32)
        keep_row = lax.dynamic_slice_in_dim(kept_tiles, index, 1, 0)[0]
        col_mask = jnp.repeat(keep_row, TILE).astype(jnp.float32)
        return jnp.dot(block * col_mask[None, :], ampl_full, precision=lax.Precision.HIGHEST)

    ladder = lax.map(one_block, jnp.arange(tile_rows, dtype=jnp.int32)).reshape(PAIRS, IJ_TOTAL)
    residual = driver.astype(jnp.float32) + ladder
    denom = vir_energy[:, None] - occ_energy[None, :]
    scaled = (residual / denom).astype(jnp.bfloat16)
    coupled = jnp.dot(scaled, occ_coupling, preferred_element_type=jnp.float32)
    return -(residual - coupled) / denom
```

```python
import jax
import jax.numpy as jnp
from jax import lax
from jax.sharding import PartitionSpec as P

LANES = 128
SCALE = 8.0


def flip(value, axes, sizes, steps):
    pairs = []
    total = 1
    for size in sizes:
        total *= size
    for source in range(total):
        rest, target, scale = source, 0, 1
        for size, step in zip(reversed(sizes), reversed(steps)):
            target += ((rest % size) ^ step) * scale
            rest //= size
            scale *= size
        pairs.append((source, target))
    return lax.ppermute(value, axes, pairs)


def halves(value, bit, axis):
    low, high = jnp.split(value, 2, axis)
    return jnp.where(bit == 0, low, high), jnp.where(bit == 0, high, low)


def chunk_bounds(columns):
    tiles = columns // (2 * LANES)
    if tiles < 2 or columns % (2 * LANES):
        return [(0, columns)]
    first = 2 * LANES * ((2 * tiles + 2) // 3)
    return [(0, first), (first, columns)]


def solution(mesh):
    rows_n, cols_n, pair_n = mesh.shape["row"], mesh.shape["col"], mesh.shape["pair"]
    chips = cols_n // 2

    def per_device(integrals, kept_tiles, amplitudes, driver, vir_energy, occ_energy, occ_coupling):
        row, col, pair = (lax.axis_index(a) for a in ("row", "col", "pair"))
        core, chip = col % 2, col // 2
        bra, kets = integrals.shape
        depth, width = amplitudes.shape
        tile = bra // kept_tiles.shape[0]
        own_rows = driver.shape[0]
        bounds = chunk_bounds(width)

        mine, others = [], []
        for low, high in bounds:
            a, b = halves(amplitudes[:, low:high], core, 1)
            mine.append(a)
            others.append(b)
        integrals_2 = flip(integrals, "col", (cols_n,), (1,))
        tiles_2 = flip(kept_tiles, "col", (cols_n,), (1,))
        near = [flip(b, "col", (cols_n,), (1,)) for b in others]
        far = []
        for a, b in zip(mine, others):
            blocks = []
            for step in range(1, rows_n):
                blocks.append(flip(a, ("row", "col"), (rows_n, cols_n), (step, 0)))
                blocks.append(flip(b, ("row", "col"), (rows_n, cols_n), (step, 1)))
            far.append(blocks)

        order = [int(format(i, f"0{chips.bit_length() - 1}b")[::-1], 2) if chips > 1 else 0 for i in range(chips)]
        group = bra // chips

        def screened(values, tiles):
            keep = jnp.repeat(tiles.astype(jnp.bfloat16) * SCALE, tile, axis=1)
            keep = jnp.repeat(keep, tile, axis=0)
            values = values * keep
            values = jnp.concatenate(
                [lax.dynamic_slice_in_dim(values, (chip ^ o) * group, group, 0) for o in order], 0
            )
            return [
                lax.dynamic_slice_in_dim(values, (row ^ step) * depth, depth, 1) for step in range(rows_n)
            ]

        first, second = screened(integrals, kept_tiles), screened(integrals_2, tiles_2)
        left = [m for pairing in zip(first, second) for m in pairing]

        def dot(a, b):
            return jnp.dot(a, b, preferred_element_type=jnp.float32)

        parts = []
        for a, b, blocks in zip(mine, near, far):
            total = dot(left[0], a) + dot(left[1], b)
            total += dot(jnp.concatenate(left[2:], 1), jnp.concatenate(blocks, 0))
            parts.append(total)

        step = 1
        while step < chips:
            for i, total in enumerate(parts):
                keep, send = jnp.split(total, 2, 0)
                got = flip(send.astype(jnp.float16), "col", (cols_n,), (2 * step,))
                parts[i] = keep + got.astype(jnp.float32)
            step *= 2

        denom = vir_energy[:, None] - occ_energy[None, :]
        coupled = jnp.zeros((own_rows, occ_energy.shape[0]), jnp.float32)
        residuals = []
        for (low, high), total in zip(bounds, parts):
            share = total.shape[1]
            blocks = total.astype(jnp.float16).reshape(2, pair_n, own_rows, share)
            by_pair = [None] * pair_n
            got = []
            for step in range(pair_n):
                sent = lax.dynamic_index_in_dim(blocks, pair ^ step, 1, False)
                got.append(sent if step == 0 else flip(sent, "pair", (pair_n,), (step,)))
            got = jnp.stack(got)
            got = jnp.stack([lax.dynamic_index_in_dim(got, pair ^ i, 0, False) for i in range(pair_n)], 1)
            keep, send = lax.dynamic_index_in_dim(got, core, 0, False), lax.dynamic_index_in_dim(got, 1 - core, 0, False)
            back = flip(send, "col", (cols_n,), (1,))
            low_half, high_half = jnp.where(core == 0, keep, back), jnp.where(core == 0, back, keep)
            for i in range(pair_n):
                ladder = jnp.concatenate([low_half[i], high_half[i]], 1).astype(jnp.float32)
                span = slice(i * width + low, i * width + high)
                residual = driver[:, span].astype(jnp.float32) + ladder * (1 / SCALE)
                scaled = (residual / denom[:, span]).astype(jnp.bfloat16)
                coupled += dot(scaled, occ_coupling[span])
                residuals.append((i, low, residual))
        residual = jnp.concatenate([r for _, _, r in sorted(residuals, key=lambda t: t[:2])], 1)
        return -(residual - coupled) / denom

    return jax.shard_map(
        per_device,
        mesh=mesh,
        in_specs=(
            P("row", "col"),
            P("row", "col"),
            P(("col", "row"), "pair"),
            P(("row", "col", "pair"), None),
            P(("row", "col", "pair")),
            P(),
            P(),
        ),
        out_specs=P(("row", "col", "pair"), None),
        check_vma=False,
    )
```

```python
import jax
import jax.numpy as jnp
from jax import lax
from jax.experimental import pallas as pl
from jax.experimental.pallas import tpu as pltpu
from jax.sharding import PartitionSpec as P


SCALE = 8.0


def flip(value, axes, sizes, steps):
    pairs = []
    total = 1
    for size in sizes:
        total *= size
    for source in range(total):
        rest, target, scale = source, 0, 1
        for size, step in zip(reversed(sizes), reversed(steps)):
            target += ((rest % size) ^ step) * scale
            rest //= size
            scale *= size
        pairs.append((source, target))
    return lax.ppermute(value, axes, pairs)


def update_kernel(ladder, driver, vir, occ, coupling, out):
    denom = vir[...] - occ[...]
    residual = driver[...].astype(jnp.float32) + ladder[...] * (1 / SCALE)
    scaled = (residual / denom).astype(jnp.bfloat16)
    coupled = jnp.dot(scaled, coupling[...], preferred_element_type=jnp.float32)
    out[...] = -(residual - coupled) / denom


def update(ladder, driver, vir_energy, occ_energy, occ_coupling):
    rows, columns = ladder.shape
    return pl.pallas_call(
        update_kernel,
        out_shape=jax.ShapeDtypeStruct((rows, columns), jnp.float32),
        compiler_params=pltpu.CompilerParams(vmem_limit_bytes=16 * 2**20),
        name="update",
    )(ladder, driver, vir_energy[:, None], occ_energy[None, :], occ_coupling)


def halves(value, bit, axis):
    low, high = jnp.split(value, 2, axis)
    return jnp.where(bit == 0, low, high), jnp.where(bit == 0, high, low)


def chunk_bounds(columns):
    return [(0, columns)]


def z_order(chips):
    return [chips // 2] + [s for s in range(1, chips) if s != chips // 2] if chips > 1 else []


def solution(mesh):
    rows_n, cols_n, pair_n = mesh.shape["row"], mesh.shape["col"], mesh.shape["pair"]
    chips = cols_n // 2

    def body(integrals, kept_tiles, amplitudes, driver, vir_energy, occ_energy, occ_coupling):
        row, col, pair = (lax.axis_index(a) for a in ("row", "col", "pair"))
        core, chip = col & 1, col >> 1
        depth, width = amplitudes.shape
        own_rows = driver.shape[0]
        bounds = chunk_bounds(width)

        mine, others = [], []
        for low, high in bounds:
            a, b = halves(amplitudes[:, low:high], core, 1)
            mine.append(a)
            others.append(b)
        far, near = [], []
        for a, b in zip(mine, others):
            blocks = []
            for step in range(1, rows_n):
                blocks.append(flip(a, ("row", "col"), (rows_n, cols_n), (step, 0)))
                blocks.append(flip(b, ("row", "col"), (rows_n, cols_n), (step, 1)))
            far.append(blocks)
        tiles_2 = flip(kept_tiles, "col", (cols_n,), (1,))
        integrals_2 = flip(integrals, "col", (cols_n,), (1,))
        for b in others:
            near.append(flip(b, "col", (cols_n,), (1,)))

        bra, tile = integrals.shape[0], integrals.shape[0] // kept_tiles.shape[0]
        group = bra // chips

        def screened(values, tiles):
            keep = jnp.repeat(tiles.astype(jnp.bfloat16) * SCALE, tile, axis=1)
            values = values * jnp.repeat(keep, tile, axis=0)
            values = jnp.concatenate(
                [lax.dynamic_slice_in_dim(values, (chip ^ o) * group, group, 0) for o in range(chips)], 0
            )
            return [lax.dynamic_slice_in_dim(values, (row ^ s) * depth, depth, 1) for s in range(rows_n)]

        first, second = screened(integrals, kept_tiles), screened(integrals_2, tiles_2)
        left = [m for pairing in zip(first, second) for m in pairing]

        def dot(a, b):
            return jnp.dot(a, b, preferred_element_type=jnp.float32)

        early = []
        for a, b in zip(mine, near):
            early.append(dot(left[0], a) + dot(left[1], b))
        parts = []
        for i, blocks in enumerate(far):
            late = dot(jnp.concatenate(left[2:], 1), jnp.concatenate(blocks, 0))
            parts.append(early[i] + late)

        for i, part in enumerate(parts):
            total = part[:group]
            for step in z_order(chips):
                send = part[step * group : (step + 1) * group].astype(jnp.float16)
                got = flip(send, "col", (cols_n,), (2 * step,))
                total += got.astype(jnp.float32)
            parts[i] = total

        share = width // 2
        blocks = jnp.concatenate([t.astype(jnp.float16) for t in parts], 1)
        blocks = blocks.reshape(2, pair_n, own_rows, share)
        got = []
        for step in range(pair_n):
            sent = lax.dynamic_index_in_dim(blocks, pair ^ step, 1, False)
            got.append(sent if step == 0 else flip(sent, "pair", (pair_n,), (step,)))
        keep = [jnp.where(core == 0, g[0], g[1]) for g in got]
        send = jnp.stack([jnp.where(core == 0, g[1], g[0]) for g in got])
        back = flip(send, "col", (cols_n,), (1,))
        columns = []
        for i in range(pair_n):
            halves_of = []
            for first_half in (True, False):
                candidates = [jnp.where((core == 0) == first_half, keep[s], back[s]) for s in range(pair_n)]
                chosen = candidates[0]
                for s in range(1, pair_n):
                    chosen = jnp.where(pair == i ^ s, candidates[s], chosen)
                halves_of.append(chosen)
            for low, high in bounds:
                columns += [h[:, low // 2 : high // 2] for h in halves_of]
        ladder = jnp.concatenate(columns, 1).astype(jnp.float32)
        return update(ladder, driver, vir_energy, occ_energy, occ_coupling)

    return jax.shard_map(
        body,
        mesh=mesh,
        in_specs=(
            P("row", "col"),
            P("row", "col"),
            P(("col", "row"), "pair"),
            P(("row", "col", "pair"), None),
            P(("row", "col", "pair")),
            P(),
            P(),
        ),
        out_specs=P(("row", "col", "pair"), None),
        check_vma=False,
    )
```

```python
import jax
import jax.numpy as jnp
from jax import lax
from jax.experimental import pallas as pl
from jax.experimental.pallas import tpu as pltpu
from jax.sharding import PartitionSpec as P


SCALE = 8.0


def flip(value, axes, sizes, steps):
    pairs = []
    total = 1
    for size in sizes:
        total *= size
    for source in range(total):
        rest, target, scale = source, 0, 1
        for size, step in zip(reversed(sizes), reversed(steps)):
            target += ((rest % size) ^ step) * scale
            rest //= size
            scale *= size
        pairs.append((source, target))
    return lax.ppermute(value, axes, pairs)


def update_kernel(ladder, driver, vir, occ, coupling, out):
    count = vir.shape[1]
    diagonal = lax.broadcasted_iota(jnp.int32, (count, count), 0) == lax.broadcasted_iota(jnp.int32, (count, count), 1)
    tall = jnp.sum(jnp.where(diagonal, vir[...], 0.0), axis=1, keepdims=True)
    denom = tall - occ[...]
    residual = driver[...].astype(jnp.float32) + ladder[...] * (1 / SCALE)
    scaled = (residual / denom).astype(jnp.bfloat16)
    coupled = jnp.dot(scaled, coupling[...], preferred_element_type=jnp.float32)
    out[...] = -(residual - coupled) / denom


def update(ladder, driver, vir_energy, occ_energy, occ_coupling):
    rows, columns = ladder.shape
    return pl.pallas_call(
        update_kernel,
        out_shape=jax.ShapeDtypeStruct((rows, columns), jnp.float32),
        compiler_params=pltpu.CompilerParams(vmem_limit_bytes=16 * 2**20),
        name="update",
    )(ladder, driver, vir_energy[None, :], occ_energy[None, :], occ_coupling)


def halves(value, first, axis):
    low, high = jnp.split(value, 2, axis)
    return jnp.where(first, low, high), jnp.where(first, high, low)


def pick(at, options):
    chosen = options[0]
    for here, option in zip(at[1:], options[1:]):
        chosen = jnp.where(here, option, chosen)
    return chosen


def chunk_bounds(columns):
    return [(0, columns)]


def z_order(chips):
    return [chips // 2] + [s for s in range(1, chips) if s != chips // 2] if chips > 1 else []


def solution(mesh):
    rows_n, cols_n, pair_n = mesh.shape["row"], mesh.shape["col"], mesh.shape["pair"]
    chips = cols_n // 2

    def body(integrals, kept_tiles, amplitudes, driver, vir_energy, occ_energy, occ_coupling):
        row, col, pair = (lax.axis_index(a) for a in ("row", "col", "pair"))
        core, chip = col & 1, col >> 1
        depth, width = amplitudes.shape
        own_rows = driver.shape[0]
        bounds = chunk_bounds(width)

        first_core = core == 0
        at_pair = [pair == i for i in range(pair_n)]
        mine, others = [], []
        for low, high in bounds:
            a, b = halves(amplitudes[:, low:high], first_core, 1)
            mine.append(a)
            others.append(b)
        mine, others, first_core, at_pair = lax.optimization_barrier((mine, others, first_core, at_pair))
        far, near = [], []
        for a, b in zip(mine, others):
            blocks = []
            for step in range(1, rows_n):
                blocks.append(flip(a, ("row", "col"), (rows_n, cols_n), (step, 0)))
                blocks.append(flip(b, ("row", "col"), (rows_n, cols_n), (step, 1)))
            far.append(blocks)
        tiles_2 = flip(kept_tiles, "col", (cols_n,), (1,))
        integrals_2 = flip(integrals, "col", (cols_n,), (1,))
        for b in others:
            near.append(flip(b, "col", (cols_n,), (1,)))

        bra, tile = integrals.shape[0], integrals.shape[0] // kept_tiles.shape[0]
        group = bra // chips

        def screened(values, tiles):
            keep = jnp.repeat(tiles.astype(jnp.bfloat16) * SCALE, tile, axis=1)
            values = values * jnp.repeat(keep, tile, axis=0)
            values = jnp.concatenate(
                [lax.dynamic_slice_in_dim(values, (chip ^ o) * group, group, 0) for o in range(chips)], 0
            )
            return [lax.dynamic_slice_in_dim(values, (row ^ s) * depth, depth, 1) for s in range(rows_n)]

        first, second = screened(integrals, kept_tiles), screened(integrals_2, tiles_2)
        left = [m for pairing in zip(first, second) for m in pairing]

        def dot(a, b):
            return jnp.dot(a, b, preferred_element_type=jnp.float32)

        early = []
        for a, b in zip(mine, near):
            early.append(dot(left[0], a) + dot(left[1], b))
        parts = []
        for i, blocks in enumerate(far):
            late = dot(jnp.concatenate(left[2:], 1), jnp.concatenate(blocks, 0))
            parts.append(early[i] + late)

        for i, part in enumerate(parts):
            total = part[:group]
            for step in z_order(chips):
                send = part[step * group : (step + 1) * group].astype(jnp.float16)
                got = flip(send, "col", (cols_n,), (2 * step,))
                total += got.astype(jnp.float32)
            parts[i] = total

        share = width // 2
        blocks = jnp.concatenate([t.astype(jnp.float16) for t in parts], 1)
        blocks = blocks.reshape(2, pair_n, own_rows, share)
        got = []
        for step in range(pair_n):
            sent = pick(at_pair, [blocks[:, i ^ step] for i in range(pair_n)])
            got.append(sent if step == 0 else flip(sent, "pair", (pair_n,), (step,)))
        keep = [jnp.where(first_core, g[0], g[1]) for g in got]
        send = jnp.stack([jnp.where(first_core, g[1], g[0]) for g in got])
        back = flip(send, "col", (cols_n,), (1,))
        columns = []
        for i in range(pair_n):
            low_core = [jnp.where(first_core, keep[s], back[s]) for s in range(pair_n)]
            high_core = [jnp.where(first_core, back[s], keep[s]) for s in range(pair_n)]
            both = [pick(at_pair, [c[i ^ p] for p in range(pair_n)]) for c in (low_core, high_core)]
            for low, high in bounds:
                columns += [h[:, low // 2 : high // 2] for h in both]
        ladder = jnp.concatenate(columns, 1).astype(jnp.float32)
        return update(ladder, driver, vir_energy, occ_energy, occ_coupling)

    return jax.shard_map(
        body,
        mesh=mesh,
        in_specs=(
            P("row", "col"),
            P("row", "col"),
            P(("col", "row"), "pair"),
            P(("row", "col", "pair"), None),
            P(("row", "col", "pair")),
            P(),
            P(),
        ),
        out_specs=P(("row", "col", "pair"), None),
        check_vma=False,
    )
```

```python
import functools

import jax
import jax.numpy as jnp
from jax import lax
from jax.experimental.layout import Layout, with_layout_constraint
from jax.experimental import pallas as pl
from jax.experimental.pallas import tpu as pltpu
from jax.sharding import PartitionSpec as P


LANES = 128
SCALE = 8.0


def flip(value, axes, sizes, steps):
    pairs = []
    total = 1
    for size in sizes:
        total *= size
    for source in range(total):
        rest, target, scale = source, 0, 1
        for size, step in zip(reversed(sizes), reversed(steps)):
            target += ((rest % size) ^ step) * scale
            rest //= size
            scale *= size
        pairs.append((source, target))
    return lax.ppermute(value, axes, pairs)


def tall(row):
    count = row.shape[1]
    diagonal = lax.broadcasted_iota(jnp.int32, (count, count), 0) == lax.broadcasted_iota(jnp.int32, (count, count), 1)
    return jnp.sum(jnp.where(diagonal, row[...], 0.0), axis=1, keepdims=True)


def spans(side, share, count):
    return [pl.ds(pl.multiple_of((2 * i + side) * share, LANES), share) for i in range(count)]


def terms(ladder, driver, vir, occ, span, i, share):
    denom = vir - occ[:, span]
    residual = driver[:, span].astype(jnp.float32) + ladder[:, i * share : (i + 1) * share] * (1 / SCALE)
    return residual, denom


def couple(ladder, driver, vir, occ, coupling, columns):
    total, share = None, ladder.shape[1] // len(columns)
    for i, span in enumerate(columns):
        residual, denom = terms(ladder, driver, vir, occ, span, i, share)
        scaled = (residual / denom).astype(jnp.bfloat16)
        product = jnp.dot(scaled, coupling[span, :], preferred_element_type=jnp.float32)
        total = product if total is None else total + product
    return total


def begin_kernel(share, ladder, driver, vir, occ, coupling, out):
    core = lax.axis_index("col") & 1
    columns = spans(core, share, ladder.shape[1] // share)
    out[...] = couple(ladder, driver, tall(vir), occ, coupling, columns)


def finish_kernel(share, mine, others, driver, vir, occ, coupling, begun, out, coupled):
    core = lax.axis_index("col") & 1
    count = mine.shape[1] // share
    here, there = spans(core, share, count), spans(1 - core, share, count)
    column = tall(vir)
    coupled[...] = begun[...] + couple(others, driver, column, occ, coupling, there)
    for ladder, columns in ((mine, here), (others, there)):
        for i, span in enumerate(columns):
            residual, denom = terms(ladder, driver, column, occ, span, i, share)
            out[:, span] = -(residual - coupled[:, span]) / denom


def update_call(kernel, rows, columns, scratch, *args):
    return pl.pallas_call(
        kernel,
        out_shape=jax.ShapeDtypeStruct((rows, columns), jnp.float32),
        scratch_shapes=scratch,
        compiler_params=pltpu.CompilerParams(vmem_limit_bytes=16 * 2**20),
    )(*args)


def fetch_kernel(share, bounds, whole, *refs):
    count = 2 * len(bounds)
    extra = (len(refs) - 1 - count) // 2
    others, outs, sems = refs[:extra], refs[extra:-1], refs[-1]
    core = lax.axis_index("col") & 1
    sources = []
    for low, high in bounds:
        for side in (core, 1 - core):
            start = pl.multiple_of(side * share + low, LANES)
            sources.append(whole.at[:, pl.ds(start, high - low)])
    sources += others
    copies = [pltpu.make_async_copy(source, out, sems.at[i]) for i, (source, out) in enumerate(zip(sources, outs))]
    for copy in copies:
        copy.start()
    for copy in copies:
        copy.wait()


def fetch(value, bounds, *others):
    rows, columns = value.shape
    shapes = [pltpu.VMEM((rows, high - low), value.dtype) for low, high in bounds for _ in range(2)]
    shapes += [pltpu.VMEM(o.shape, o.dtype) for o in others]
    outs = pl.pallas_call(
        functools.partial(fetch_kernel, columns // 2, bounds),
        out_shape=shapes,
        in_specs=[pl.BlockSpec(memory_space=pltpu.HBM)] * (1 + len(others)),
        out_specs=[pl.BlockSpec(memory_space=pltpu.VMEM)] * len(shapes),
        scratch_shapes=[pltpu.SemaphoreType.DMA((len(shapes),))],
        compiler_params=pltpu.CompilerParams(vmem_limit_bytes=4 * 2**20),
        name="fetch",
    )(*[pltpu.with_memory_space_constraint(v, pltpu.HBM) for v in (value, *others)])
    count = 2 * len(bounds)
    return outs[0:count:2], outs[1:count:2]


def pick(at, options):
    chosen = options[0]
    for here, option in zip(at[1:], options[1:]):
        chosen = jnp.where(here, option, chosen)
    return chosen


FIRST = 2
EARLY = "21"
REST = ((2, 1), (3, None), (1, 1))


def chunk_bounds(share):
    first = FIRST * LANES
    return [(0, first), (first, share)] if first < share else [(0, share)]


def sends(chips, chunks):
    if chips == 4 and chunks == 2:
        return [(int(e), 0) for e in EARLY] + list(REST)
    steps = sorted(range(1, chips), key=lambda s: (s != chips // 2, s))
    return [(s, None) for s in steps]


def solution(mesh):
    rows_n, cols_n, pair_n = mesh.shape["row"], mesh.shape["col"], mesh.shape["pair"]
    chips = cols_n // 2

    def body(integrals, kept_tiles, amplitudes, driver, vir_energy, occ_energy, occ_coupling):
        row, col, pair = (lax.axis_index(a) for a in ("row", "col", "pair"))
        core, chip = col & 1, col >> 1
        depth, width = amplitudes.shape
        own_rows = driver.shape[0]
        share = width // 2
        bounds = chunk_bounds(share)

        first_core = core == 0
        at_pair = [pair == i for i in range(pair_n)]
        mine, others = fetch(amplitudes, bounds)
        mine, others, first_core, at_pair = lax.optimization_barrier((list(mine), list(others), first_core, at_pair))
        far, near = [], []
        for a, b in zip(mine, others):
            blocks = []
            for step in range(1, rows_n):
                blocks.append(flip(a, ("row", "col"), (rows_n, cols_n), (step, 0)))
                blocks.append(flip(b, ("row", "col"), (rows_n, cols_n), (step, 1)))
            far.append(blocks)
        tiles_2 = flip(kept_tiles, "col", (cols_n,), (1,))
        integrals_2 = flip(integrals, "col", (cols_n,), (1,))
        for b in others:
            near.append(flip(b, "col", (cols_n,), (1,)))

        bra, tile = integrals.shape[0], integrals.shape[0] // kept_tiles.shape[0]
        group = bra // chips

        def screened(values, tiles):
            keep = jnp.repeat(tiles.astype(jnp.bfloat16) * SCALE, tile, axis=1)
            values = values * jnp.repeat(keep, tile, axis=0)
            values = jnp.concatenate(
                [lax.dynamic_slice_in_dim(values, (chip ^ o) * group, group, 0) for o in range(chips)], 0
            )
            return [lax.dynamic_slice_in_dim(values, (row ^ s) * depth, depth, 1) for s in range(rows_n)]

        first, second = screened(integrals, kept_tiles), screened(integrals_2, tiles_2)
        left = [m for pairing in zip(first, second) for m in pairing]

        def dot(a, b):
            return with_layout_constraint(jnp.dot(a, b, preferred_element_type=jnp.float32), Layout((0, 1)))

        early = []
        for a, b in zip(mine, near):
            early.append(dot(left[0], a) + dot(left[1], b))
        parts, halved = [], []
        for i, blocks in enumerate(far):
            late = dot(jnp.concatenate(left[2:], 1), jnp.concatenate(blocks, 0))
            parts.append(early[i] + late)
            halved.append(parts[-1].astype(jnp.float16))

        def rows_for(value, step):
            return value[step * group : (step + 1) * group]

        totals = [rows_for(p, 0) for p in parts]
        for step, chunk in sends(chips, len(bounds)):
            if chunk is None:
                sent = jnp.concatenate([rows_for(h, step) for h in halved], 1)
            else:
                sent = rows_for(halved[chunk], step)
            got = flip(sent, "col", (cols_n,), (2 * step,))
            if chunk is None:
                got = [got[:, low:high].astype(jnp.float32) for low, high in bounds]
                totals = [t + g for t, g in zip(totals, got)]
            else:
                totals[chunk] += got.astype(jnp.float32)
        total = jnp.concatenate([t.astype(jnp.float16) for t in totals], 1)

        blocks = total.reshape(2, pair_n, own_rows, share)
        got = []
        for step in range(pair_n):
            sent = pick(at_pair, [blocks[:, i ^ step] for i in range(pair_n)])
            got.append(sent if step == 0 else flip(sent, "pair", (pair_n,), (step,)))
        keep = [jnp.where(first_core, g[0], g[1]) for g in got]
        send = jnp.stack([jnp.where(first_core, g[1], g[0]) for g in got])
        back = flip(send, "col", (cols_n,), (1,))

        def in_order(values):
            parts = [pick(at_pair, [values[i ^ p] for p in range(pair_n)]) for i in range(pair_n)]
            return jnp.concatenate(parts, 1).astype(jnp.float32)

        rest = (driver, vir_energy[None, :], occ_energy[None, :], occ_coupling)
        columns = occ_energy.shape[0]
        here = in_order(keep)
        begun = update_call(functools.partial(begin_kernel, share), own_rows, columns, [], here, *rest)
        there = in_order(back)
        scratch = [pltpu.VMEM((own_rows, columns), jnp.float32)]
        kernel = functools.partial(finish_kernel, share)
        return update_call(kernel, own_rows, columns, scratch, here, there, *rest, begun)

    return jax.shard_map(
        body,
        mesh=mesh,
        in_specs=(
            P("row", "col"),
            P("row", "col"),
            P(("col", "row"), "pair"),
            P(("row", "col", "pair"), None),
            P(("row", "col", "pair")),
            P(),
            P(),
        ),
        out_specs=P(("row", "col", "pair"), None),
        check_vma=False,
    )
```

```python
import functools

import jax
import jax.numpy as jnp
from jax import lax
from jax.experimental.layout import Layout, with_layout_constraint
from jax.experimental import pallas as pl
from jax.experimental.pallas import tpu as pltpu
from jax.sharding import PartitionSpec as P


LANES = 128
SCALE = 8.0


def flip(value, axes, sizes, steps):
    pairs = []
    total = 1
    for size in sizes:
        total *= size
    for source in range(total):
        rest, target, scale = source, 0, 1
        for size, step in zip(reversed(sizes), reversed(steps)):
            target += ((rest % size) ^ step) * scale
            rest //= size
            scale *= size
        pairs.append((source, target))
    return lax.ppermute(value, axes, pairs)


def tall(row):
    count = row.shape[1]
    diagonal = lax.broadcasted_iota(jnp.int32, (count, count), 0) == lax.broadcasted_iota(jnp.int32, (count, count), 1)
    return jnp.sum(jnp.where(diagonal, row[...], 0.0), axis=1, keepdims=True)


def terms(piece, share, ladder, driver, vir, occ):
    mine, low, high = piece
    size = high - low
    core = lax.axis_index("col") & 1
    side = core if mine else 1 - core
    for i in range(ladder.shape[1] // size):
        span = pl.ds(pl.multiple_of((2 * i + side) * share + low, LANES), size)
        residual = driver[:, span].astype(jnp.float32) + ladder[:, i * size : (i + 1) * size] * (1 / SCALE)
        yield span, residual, vir - occ[:, span]


def couple(total, pieces, share, ladders, driver, vir, occ, coupling):
    for piece, ladder in zip(pieces, ladders):
        for span, residual, denom in terms(piece, share, ladder, driver, vir, occ):
            scaled = (residual / denom).astype(jnp.bfloat16)
            product = jnp.dot(scaled, coupling[span, :], preferred_element_type=jnp.float32)
            total = product if total is None else total + product
    return total


def begin_kernel(pieces, share, carried, driver, vir, occ, coupling, *refs):
    ladders, out = refs[: len(pieces)], refs[-1]
    total = refs[len(pieces)][...] if carried else None
    out[...] = couple(total, pieces, share, ladders, driver, tall(vir), occ, coupling)


def finish_kernel(pieces, share, last, driver, vir, occ, coupling, *refs):
    ladders, begun, out, coupled = refs[: len(pieces)], *refs[len(pieces) :]
    column = tall(vir)
    coupled[...] = couple(begun[...], pieces[last:], share, ladders[last:], driver, column, occ, coupling)
    for piece, ladder in zip(pieces, ladders):
        for span, residual, denom in terms(piece, share, ladder, driver, column, occ):
            out[:, span] = -(residual - coupled[:, span]) / denom


def update_call(kernel, rows, columns, scratch, *args):
    return pl.pallas_call(
        kernel,
        out_shape=jax.ShapeDtypeStruct((rows, columns), jnp.float32),
        scratch_shapes=scratch,
        compiler_params=pltpu.CompilerParams(vmem_limit_bytes=16 * 2**20),
    )(*args)


def fetch_kernel(share, bounds, whole, *refs):
    count = 2 * len(bounds)
    extra = (len(refs) - 1 - count) // 2
    others, outs, sems = refs[:extra], refs[extra:-1], refs[-1]
    core = lax.axis_index("col") & 1
    sources = []
    for low, high in bounds:
        for side in (core, 1 - core):
            start = pl.multiple_of(side * share + low, LANES)
            sources.append(whole.at[:, pl.ds(start, high - low)])
    sources += others
    copies = [pltpu.make_async_copy(source, out, sems.at[i]) for i, (source, out) in enumerate(zip(sources, outs))]
    for copy in copies:
        copy.start()
    for copy in copies:
        copy.wait()


def fetch(value, bounds, *others):
    rows, columns = value.shape
    shapes = [pltpu.VMEM((rows, high - low), value.dtype) for low, high in bounds for _ in range(2)]
    shapes += [pltpu.VMEM(o.shape, o.dtype) for o in others]
    outs = pl.pallas_call(
        functools.partial(fetch_kernel, columns // 2, bounds),
        out_shape=shapes,
        in_specs=[pl.BlockSpec(memory_space=pltpu.HBM)] * (1 + len(others)),
        out_specs=[pl.BlockSpec(memory_space=pltpu.VMEM)] * len(shapes),
        scratch_shapes=[pltpu.SemaphoreType.DMA((len(shapes),))],
        compiler_params=pltpu.CompilerParams(vmem_limit_bytes=4 * 2**20),
        name="fetch",
    )(*[pltpu.with_memory_space_constraint(v, pltpu.HBM) for v in (value, *others)])
    count = 2 * len(bounds)
    return outs[0:count:2], outs[1:count:2]


def pick(at, options):
    chosen = options[0]
    for here, option in zip(at[1:], options[1:]):
        chosen = jnp.where(here, option, chosen)
    return chosen


FIRST = 2
EARLY = "213"
REST = ((2, 1), (3, 1), (1, 1))


def chunk_bounds(share):
    first = FIRST * LANES
    return [(0, first), (first, share)] if first < share else [(0, share)]


def sends(chips, chunks):
    if chips == 4 and chunks == 2:
        return [(int(e), 0) for e in EARLY] + list(REST)
    steps = sorted(range(1, chips), key=lambda s: (s != chips // 2, s))
    return [(s, None) for s in steps]


def solution(mesh):
    rows_n, cols_n, pair_n = mesh.shape["row"], mesh.shape["col"], mesh.shape["pair"]
    chips = cols_n // 2

    def body(integrals, kept_tiles, amplitudes, driver, vir_energy, occ_energy, occ_coupling):
        row, col, pair = (lax.axis_index(a) for a in ("row", "col", "pair"))
        core, chip = col & 1, col >> 1
        depth, width = amplitudes.shape
        own_rows = driver.shape[0]
        share = width // 2
        bounds = chunk_bounds(share)

        first_core = core == 0
        at_pair = [pair == i for i in range(pair_n)]
        mine, others = fetch(amplitudes, bounds)
        mine, others, first_core, at_pair = lax.optimization_barrier((list(mine), list(others), first_core, at_pair))
        far, near = [], []
        for a, b in zip(mine, others):
            blocks = []
            for step in range(1, rows_n):
                blocks.append(flip(a, ("row", "col"), (rows_n, cols_n), (step, 0)))
                blocks.append(flip(b, ("row", "col"), (rows_n, cols_n), (step, 1)))
            far.append(blocks)
        tiles_2 = flip(kept_tiles, "col", (cols_n,), (1,))
        integrals_2 = flip(integrals, "col", (cols_n,), (1,))
        for b in others:
            near.append(flip(b, "col", (cols_n,), (1,)))

        bra, tile = integrals.shape[0], integrals.shape[0] // kept_tiles.shape[0]
        group = bra // chips

        def screened(values, tiles):
            keep = jnp.repeat(tiles.astype(jnp.bfloat16) * SCALE, tile, axis=1)
            values = values * jnp.repeat(keep, tile, axis=0)
            values = jnp.concatenate(
                [lax.dynamic_slice_in_dim(values, (chip ^ o) * group, group, 0) for o in range(chips)], 0
            )
            return [lax.dynamic_slice_in_dim(values, (row ^ s) * depth, depth, 1) for s in range(rows_n)]

        first, second = screened(integrals, kept_tiles), screened(integrals_2, tiles_2)
        left = [m for pairing in zip(first, second) for m in pairing]

        def dot(a, b):
            return with_layout_constraint(jnp.dot(a, b, preferred_element_type=jnp.float32), Layout((0, 1)))

        near_left, far_left = jnp.concatenate(left[:2], 1), jnp.concatenate(left[2:], 1)
        early = []
        for a, b in zip(mine, near):
            early.append(dot(near_left, jnp.concatenate([a, b], 0)))
        early, far[0] = lax.optimization_barrier((early, far[0]))
        parts, halved = [], []
        for i, blocks in enumerate(far):
            late = dot(far_left, jnp.concatenate(blocks, 0))
            parts.append(early[i] + late)
            halved.append(parts[-1].astype(jnp.float16))

        def rows_for(value, step):
            return value[step * group : (step + 1) * group]

        totals = [rows_for(p, 0) for p in parts]
        arrived = [[] for _ in parts]
        for step, chunk in sends(chips, len(bounds)):
            if chunk is None:
                sent = jnp.concatenate([rows_for(h, step) for h in halved], 1)
            else:
                sent = rows_for(halved[chunk], step)
            got = flip(sent, "col", (cols_n,), (2 * step,))
            if chunk is None:
                for i, (low, high) in enumerate(bounds):
                    arrived[i].append(got[:, low:high])
            else:
                arrived[chunk].append(got)

        rest = (driver, vir_energy[None, :], occ_energy[None, :], occ_coupling)
        pieces, ladders = [], []
        for c, (low, high) in enumerate(bounds):
            total = totals[c]
            for value in arrived[c]:
                total += value.astype(jnp.float32)
            blocks = total.astype(jnp.float16).reshape(2, pair_n, own_rows, high - low)
            outgoing = [pick(at_pair, [blocks[:, i ^ s] for i in range(pair_n)]) for s in range(pair_n)]
            got = outgoing[:1]
            for step in range(1, pair_n):
                got.append(flip(outgoing[step], "pair", (pair_n,), (step,)))
            keep = [jnp.where(first_core, g[0], g[1]) for g in got]
            send = jnp.stack([jnp.where(first_core, g[1], g[0]) for g in got])
            back = flip(send, "col", (cols_n,), (1,))
            for mine_side, values in ((True, keep), (False, back)):
                in_order = [pick(at_pair, [values[i ^ p] for p in range(pair_n)]) for i in range(pair_n)]
                ladders.append(jnp.concatenate(in_order, 1).astype(jnp.float32))
                pieces.append((mine_side, low, high))

        columns = occ_energy.shape[0]
        begun, done = None, 0
        for c in range(len(bounds)):
            upto = 2 * c + 1
            kernel = functools.partial(begin_kernel, tuple(pieces[done:upto]), share, begun is not None)
            carried = [] if begun is None else [begun]
            begun = update_call(kernel, own_rows, columns, [], *rest, *ladders[done:upto], *carried)
            done = upto
        kernel = functools.partial(finish_kernel, tuple(pieces), share, done)
        scratch = [pltpu.VMEM((own_rows, columns), jnp.float32)]
        return update_call(kernel, own_rows, columns, scratch, *rest, *ladders, begun)

    return jax.shard_map(
        body,
        mesh=mesh,
        in_specs=(
            P("row", "col"),
            P("row", "col"),
            P(("col", "row"), "pair"),
            P(("row", "col", "pair"), None),
            P(("row", "col", "pair")),
            P(),
            P(),
        ),
        out_specs=P(("row", "col", "pair"), None),
        check_vma=False,
    )
```

```python
import functools

import jax
import jax.numpy as jnp
from jax import lax
from jax.experimental.layout import Layout, with_layout_constraint
from jax.experimental import pallas as pl
from jax.experimental.pallas import tpu as pltpu
from jax.sharding import PartitionSpec as P


LANES = 128
SCALE = 8.0


def flip(value, axes, sizes, steps):
    pairs = []
    total = 1
    for size in sizes:
        total *= size
    for source in range(total):
        rest, target, scale = source, 0, 1
        for size, step in zip(reversed(sizes), reversed(steps)):
            target += ((rest % size) ^ step) * scale
            rest //= size
            scale *= size
        pairs.append((source, target))
    return lax.ppermute(value, axes, pairs)


def tall(row):
    count = row.shape[1]
    diagonal = lax.broadcasted_iota(jnp.int32, (count, count), 0) == lax.broadcasted_iota(jnp.int32, (count, count), 1)
    return jnp.sum(jnp.where(diagonal, row[...], 0.0), axis=1, keepdims=True)


def terms(piece, share, ladder, driver, vir, occ):
    mine, step, low, high = piece
    core, pair = lax.axis_index("col") & 1, lax.axis_index("pair")
    part = 2 * (pair ^ step) + (core if mine else 1 - core)
    span = pl.ds(pl.multiple_of(part * share + low, LANES), high - low)
    residual = driver[:, span].astype(jnp.float32) + ladder[...] * (1 / SCALE)
    return span, residual, vir - occ[:, span]


def couple(total, pieces, share, ladders, driver, vir, occ, coupling):
    for piece, ladder in zip(pieces, ladders):
        span, residual, denom = terms(piece, share, ladder, driver, vir, occ)
        scaled = (residual / denom).astype(jnp.bfloat16)
        product = jnp.dot(scaled, coupling[span, :], preferred_element_type=jnp.float32)
        total = product if total is None else total + product
    return total


def begin_kernel(pieces, share, carried, driver, vir, occ, coupling, *refs):
    ladders, out = refs[: len(pieces)], refs[-1]
    total = refs[len(pieces)][...] if carried else None
    out[...] = couple(total, pieces, share, ladders, driver, tall(vir), occ, coupling)


def finish_kernel(pieces, share, last, driver, vir, occ, coupling, *refs):
    ladders, begun, out, coupled = refs[: len(pieces)], *refs[len(pieces) :]
    column = tall(vir)
    coupled[...] = couple(begun[...], pieces[last:], share, ladders[last:], driver, column, occ, coupling)
    for piece, ladder in zip(pieces, ladders):
        span, residual, denom = terms(piece, share, ladder, driver, column, occ)
        out[:, span] = -(residual - coupled[:, span]) / denom


def update_call(kernel, rows, columns, scratch, *args):
    return pl.pallas_call(
        kernel,
        out_shape=jax.ShapeDtypeStruct((rows, columns), jnp.float32),
        scratch_shapes=scratch,
        compiler_params=pltpu.CompilerParams(vmem_limit_bytes=16 * 2**20),
    )(*args)


def fetch_kernel(share, bounds, whole, *refs):
    count = 2 * len(bounds)
    extra = (len(refs) - 1 - count) // 2
    others, outs, sems = refs[:extra], refs[extra:-1], refs[-1]
    core = lax.axis_index("col") & 1
    sources = []
    for low, high in bounds:
        for side in (core, 1 - core):
            start = pl.multiple_of(side * share + low, LANES)
            sources.append(whole.at[:, pl.ds(start, high - low)])
    sources += others
    copies = [pltpu.make_async_copy(source, out, sems.at[i]) for i, (source, out) in enumerate(zip(sources, outs))]
    for copy in copies:
        copy.start()
    for copy in copies:
        copy.wait()


def fetch(value, bounds, *others):
    rows, columns = value.shape
    shapes = [pltpu.VMEM((rows, high - low), value.dtype) for low, high in bounds for _ in range(2)]
    shapes += [pltpu.VMEM(o.shape, o.dtype) for o in others]
    outs = pl.pallas_call(
        functools.partial(fetch_kernel, columns // 2, bounds),
        out_shape=shapes,
        in_specs=[pl.BlockSpec(memory_space=pltpu.HBM)] * (1 + len(others)),
        out_specs=[pl.BlockSpec(memory_space=pltpu.VMEM)] * len(shapes),
        scratch_shapes=[pltpu.SemaphoreType.DMA((len(shapes),))],
        compiler_params=pltpu.CompilerParams(vmem_limit_bytes=4 * 2**20),
        name="fetch",
    )(*[pltpu.with_memory_space_constraint(v, pltpu.HBM) for v in (value, *others)])
    count = 2 * len(bounds)
    return outs[0:count:2], outs[1:count:2]


def pick(at, options):
    chosen = options[0]
    for here, option in zip(at[1:], options[1:]):
        chosen = jnp.where(here, option, chosen)
    return chosen


FIRST = 2
EARLY = "213"
REST = ((2, 1), (3, 1), (1, 1))


def chunk_bounds(share):
    first = FIRST * LANES
    return [(0, first), (first, share)] if first < share else [(0, share)]


def sends(chips, chunks):
    if chips == 4 and chunks == 2:
        return [(int(e), 0) for e in EARLY] + list(REST)
    steps = sorted(range(1, chips), key=lambda s: (s != chips // 2, s))
    return [(s, None) for s in steps]


def solution(mesh):
    rows_n, cols_n, pair_n = mesh.shape["row"], mesh.shape["col"], mesh.shape["pair"]
    chips = cols_n // 2

    def body(integrals, kept_tiles, amplitudes, driver, vir_energy, occ_energy, occ_coupling):
        row, col, pair = (lax.axis_index(a) for a in ("row", "col", "pair"))
        core, chip = col & 1, col >> 1
        depth, width = amplitudes.shape
        own_rows = driver.shape[0]
        share = width // 2
        bounds = chunk_bounds(share)

        first_core = core == 0
        at_pair = [pair == i for i in range(pair_n)]
        mine, others = fetch(amplitudes, bounds)
        mine, others, first_core, at_pair = lax.optimization_barrier((list(mine), list(others), first_core, at_pair))
        far, near = [], []
        for a, b in zip(mine, others):
            blocks = []
            for step in range(1, rows_n):
                blocks.append(flip(a, ("row", "col"), (rows_n, cols_n), (step, 0)))
                blocks.append(flip(b, ("row", "col"), (rows_n, cols_n), (step, 1)))
            far.append(blocks)
        tiles_2 = flip(kept_tiles, "col", (cols_n,), (1,))
        integrals_2 = flip(integrals, "col", (cols_n,), (1,))
        for b in others:
            near.append(flip(b, "col", (cols_n,), (1,)))

        bra, tile = integrals.shape[0], integrals.shape[0] // kept_tiles.shape[0]
        group = bra // chips

        def screened(values, tiles):
            keep = jnp.repeat(tiles.astype(jnp.bfloat16) * SCALE, tile, axis=1)
            values = values * jnp.repeat(keep, tile, axis=0)
            values = jnp.concatenate(
                [lax.dynamic_slice_in_dim(values, (chip ^ o) * group, group, 0) for o in range(chips)], 0
            )
            return [lax.dynamic_slice_in_dim(values, (row ^ s) * depth, depth, 1) for s in range(rows_n)]

        first, second = screened(integrals, kept_tiles), screened(integrals_2, tiles_2)
        left = [m for pairing in zip(first, second) for m in pairing]

        def dot(a, b):
            return with_layout_constraint(jnp.dot(a, b, preferred_element_type=jnp.float32), Layout((0, 1)))

        near_left, far_left = jnp.concatenate(left[:2], 1), jnp.concatenate(left[2:], 1)
        early = []
        for a, b in zip(mine, near):
            early.append(dot(near_left, jnp.concatenate([a, b], 0)))
        early, far[0] = lax.optimization_barrier((early, far[0]))
        parts, halved = [], []
        for i, blocks in enumerate(far):
            late = dot(far_left, jnp.concatenate(blocks, 0))
            parts.append(early[i] + late)
            halved.append(parts[-1].astype(jnp.float16))

        def rows_for(value, step):
            return value[step * group : (step + 1) * group]

        totals = [rows_for(p, 0) for p in parts]
        arrived = [[] for _ in parts]
        for step, chunk in sends(chips, len(bounds)):
            if chunk is None:
                sent = jnp.concatenate([rows_for(h, step) for h in halved], 1)
            else:
                sent = rows_for(halved[chunk], step)
            got = flip(sent, "col", (cols_n,), (2 * step,))
            if chunk is None:
                for i, (low, high) in enumerate(bounds):
                    arrived[i].append(got[:, low:high])
            else:
                arrived[chunk].append(got)

        rest = (driver, vir_energy[None, :], occ_energy[None, :], occ_coupling)
        stages = [[], [], []]
        for c, (low, high) in enumerate(bounds):
            final = c == len(bounds) - 1
            total = totals[c]
            for value in arrived[c]:
                total += value.astype(jnp.float32)
            blocks = total.astype(jnp.float16).reshape(2, pair_n, own_rows, high - low)
            outgoing = [pick(at_pair, [blocks[:, i ^ s] for i in range(pair_n)]) for s in range(pair_n)]
            own = [jnp.where(first_core, o[0], o[1]) for o in outgoing]
            cross = [jnp.where(first_core, o[1], o[0]) for o in outgoing]

            def add(stage, mine_side, step, value):
                stages[stage].append(((mine_side, step, low, high), value.astype(jnp.float32)))

            add(0, True, 0, own[0])
            if final:
                add(1, False, 0, flip(cross[0], "col", (cols_n,), (1,)))
                for step in range(1, pair_n):
                    add(2, True, step, flip(own[step], "pair", (pair_n,), (step,)))
                for step in range(1, pair_n):
                    got = flip(cross[step], ("col", "pair"), (cols_n, pair_n), (1, step))
                    add(2, False, step, got)
            else:
                send = [cross[0]]
                for step in range(1, pair_n):
                    got = flip(outgoing[step], "pair", (pair_n,), (step,))
                    add(0, True, step, jnp.where(first_core, got[0], got[1]))
                    send.append(jnp.where(first_core, got[1], got[0]))
                back = flip(jnp.stack(send), "col", (cols_n,), (1,))
                for step in range(pair_n):
                    add(1, False, step, back[step])

        columns = occ_energy.shape[0]
        begun = None
        for c in range(2):
            kernel = functools.partial(begin_kernel, tuple(p for p, _ in stages[c]), share, begun is not None)
            carried = [] if begun is None else [begun]
            begun = update_call(kernel, own_rows, columns, [], *rest, *(v for _, v in stages[c]), *carried)
        pieces = sum(stages, [])
        last = len(stages[0]) + len(stages[1])
        kernel = functools.partial(finish_kernel, tuple(p for p, _ in pieces), share, last)
        scratch = [pltpu.VMEM((own_rows, columns), jnp.float32)]
        ladders = [v for _, v in pieces]
        return update_call(kernel, own_rows, columns, scratch, *rest, *ladders, begun)

    return jax.shard_map(
        body,
        mesh=mesh,
        in_specs=(
            P("row", "col"),
            P("row", "col"),
            P(("col", "row"), "pair"),
            P(("row", "col", "pair"), None),
            P(("row", "col", "pair")),
            P(),
            P(),
        ),
        out_specs=P(("row", "col", "pair"), None),
        check_vma=False,
    )
```

```python
import functools

import jax
import jax.numpy as jnp
from jax import lax
from jax.experimental.layout import Layout, with_layout_constraint
from jax.experimental import pallas as pl
from jax.experimental.pallas import tpu as pltpu
from jax.sharding import PartitionSpec as P


LANES = 128
SCALE = 8.0


def flip(value, axes, sizes, steps):
    pairs = []
    total = 1
    for size in sizes:
        total *= size
    for source in range(total):
        rest, target, scale = source, 0, 1
        for size, step in zip(reversed(sizes), reversed(steps)):
            target += ((rest % size) ^ step) * scale
            rest //= size
            scale *= size
        pairs.append((source, target))
    return lax.ppermute(value, axes, pairs)


def tall(row):
    count = row.shape[1]
    diagonal = lax.broadcasted_iota(jnp.int32, (count, count), 0) == lax.broadcasted_iota(jnp.int32, (count, count), 1)
    return jnp.sum(jnp.where(diagonal, row[...], 0.0), axis=1, keepdims=True)


def terms(piece, share, ladder, driver, vir, occ):
    mine, step, low, high = piece
    core, pair = lax.axis_index("col") & 1, lax.axis_index("pair")
    part = 2 * (pair ^ step) + (core if mine else 1 - core)
    span = pl.ds(pl.multiple_of(part * share + low, LANES), high - low)
    residual = driver[:, span].astype(jnp.float32) + ladder[...] * (1 / SCALE)
    return span, residual, vir - occ[:, span]


def couple(total, pieces, share, ladders, driver, vir, occ, coupling):
    for piece, ladder in zip(pieces, ladders):
        span, residual, denom = terms(piece, share, ladder, driver, vir, occ)
        scaled = (residual / denom).astype(jnp.bfloat16)
        product = jnp.dot(scaled, coupling[span, :], preferred_element_type=jnp.float32)
        total = product if total is None else total + product
    return total


def begin_kernel(pieces, share, carried, driver, vir, occ, coupling, *refs):
    ladders, out = refs[: len(pieces)], refs[-1]
    total = refs[len(pieces)][...] if carried else None
    out[...] = couple(total, pieces, share, ladders, driver, tall(vir), occ, coupling)


def finish_kernel(pieces, share, last, driver, vir, occ, coupling, *refs):
    ladders, begun, out, coupled = refs[: len(pieces)], *refs[len(pieces) :]
    column = tall(vir)
    coupled[...] = couple(begun[...], pieces[last:], share, ladders[last:], driver, column, occ, coupling)
    for piece, ladder in zip(pieces, ladders):
        span, residual, denom = terms(piece, share, ladder, driver, column, occ)
        out[:, span] = -(residual - coupled[:, span]) / denom


def update_call(kernel, rows, columns, scratch, *args):
    return pl.pallas_call(
        kernel,
        out_shape=jax.ShapeDtypeStruct((rows, columns), jnp.float32),
        scratch_shapes=scratch,
        compiler_params=pltpu.CompilerParams(vmem_limit_bytes=16 * 2**20),
    )(*args)


def fetch_kernel(share, bounds, whole, *refs):
    count = 2 * len(bounds)
    extra = (len(refs) - 1 - count) // 2
    others, outs, sems = refs[:extra], refs[extra:-1], refs[-1]
    core = lax.axis_index("col") & 1
    sources = []
    for low, high in bounds:
        for side in (core, 1 - core):
            start = pl.multiple_of(side * share + low, LANES)
            sources.append(whole.at[:, pl.ds(start, high - low)])
    sources += others
    copies = [pltpu.make_async_copy(source, out, sems.at[i]) for i, (source, out) in enumerate(zip(sources, outs))]
    for copy in copies:
        copy.start()
    for copy in copies:
        copy.wait()


def fetch(value, bounds, *others):
    rows, columns = value.shape
    shapes = [pltpu.VMEM((rows, high - low), value.dtype) for low, high in bounds for _ in range(2)]
    shapes += [pltpu.VMEM(o.shape, o.dtype) for o in others]
    outs = pl.pallas_call(
        functools.partial(fetch_kernel, columns // 2, bounds),
        out_shape=shapes,
        in_specs=[pl.BlockSpec(memory_space=pltpu.HBM)] * (1 + len(others)),
        out_specs=[pl.BlockSpec(memory_space=pltpu.VMEM)] * len(shapes),
        scratch_shapes=[pltpu.SemaphoreType.DMA((len(shapes),))],
        compiler_params=pltpu.CompilerParams(vmem_limit_bytes=4 * 2**20),
        name="fetch",
    )(*[pltpu.with_memory_space_constraint(v, pltpu.HBM) for v in (value, *others)])
    count = 2 * len(bounds)
    return outs[0:count:2], outs[1:count:2], *outs[count:]


def pick(at, options):
    chosen = options[0]
    for here, option in zip(at[1:], options[1:]):
        chosen = jnp.where(here, option, chosen)
    return chosen


FIRST = 2
EARLY = "213"
REST = ((2, 1), (3, 1), (1, 1))


def chunk_bounds(share):
    first = FIRST * LANES
    return [(0, first), (first, share)] if first < share else [(0, share)]


def sends(chips, chunks):
    if chips == 4 and chunks == 2:
        return [(int(e), 0) for e in EARLY] + list(REST)
    steps = sorted(range(1, chips), key=lambda s: (s != chips // 2, s))
    return [(s, None) for s in steps]


def solution(mesh):
    rows_n, cols_n, pair_n = mesh.shape["row"], mesh.shape["col"], mesh.shape["pair"]
    chips = cols_n // 2

    def body(integrals, kept_tiles, amplitudes, driver, vir_energy, occ_energy, occ_coupling):
        row, col, pair = (lax.axis_index(a) for a in ("row", "col", "pair"))
        core, chip = col & 1, col >> 1
        depth, width = amplitudes.shape
        own_rows = driver.shape[0]
        share = width // 2
        bounds = chunk_bounds(share)

        first_core = core == 0
        at_pair = [pair == i for i in range(pair_n)]
        mine, others, kept_tiles = fetch(amplitudes, bounds, kept_tiles)
        mine, others, first_core, at_pair = lax.optimization_barrier((list(mine), list(others), first_core, at_pair))
        far, near = [], []
        for a, b in zip(mine, others):
            blocks = []
            for step in range(1, rows_n):
                blocks.append(flip(a, ("row", "col"), (rows_n, cols_n), (step, 0)))
                blocks.append(flip(b, ("row", "col"), (rows_n, cols_n), (step, 1)))
            far.append(blocks)
        tiles_2 = flip(kept_tiles, "col", (cols_n,), (1,))
        integrals_2 = flip(integrals, "col", (cols_n,), (1,))
        for b in others:
            near.append(flip(b, "col", (cols_n,), (1,)))

        bra, tile = integrals.shape[0], integrals.shape[0] // kept_tiles.shape[0]
        group = bra // chips

        def screened(values, tiles):
            keep = jnp.repeat(tiles.astype(jnp.bfloat16) * SCALE, tile, axis=1)
            values = values * jnp.repeat(keep, tile, axis=0)
            values = jnp.concatenate(
                [lax.dynamic_slice_in_dim(values, (chip ^ o) * group, group, 0) for o in range(chips)], 0
            )
            return [lax.dynamic_slice_in_dim(values, (row ^ s) * depth, depth, 1) for s in range(rows_n)]

        first, second = screened(integrals, kept_tiles), screened(integrals_2, tiles_2)
        left = [m for pairing in zip(first, second) for m in pairing]

        def dot(a, b):
            return with_layout_constraint(jnp.dot(a, b, preferred_element_type=jnp.float32), Layout((0, 1)))

        near_left, far_left = jnp.concatenate(left[:2], 1), jnp.concatenate(left[2:], 1)
        early = []
        for a, b in zip(mine, near):
            early.append(dot(near_left, jnp.concatenate([a, b], 0)))
        early, far[0][0] = lax.optimization_barrier((early, far[0][0]))
        early[0] = early[0] + dot(left[2], far[0][0])
        early[0], far[0][1] = lax.optimization_barrier((early[0], far[0][1]))
        parts, halved = [], []
        for i, blocks in enumerate(far):
            if i:
                late = dot(far_left, jnp.concatenate(blocks, 0))
            else:
                late = dot(jnp.concatenate(left[3:], 1), jnp.concatenate(blocks[1:], 0))
            parts.append(early[i] + late)
            halved.append(parts[-1].astype(jnp.float16))

        def rows_for(value, step):
            return value[step * group : (step + 1) * group]

        totals = [rows_for(p, 0) for p in parts]
        arrived = [[] for _ in parts]
        for step, chunk in sends(chips, len(bounds)):
            if chunk is None:
                sent = jnp.concatenate([rows_for(h, step) for h in halved], 1)
            else:
                sent = rows_for(halved[chunk], step)
            got = flip(sent, "col", (cols_n,), (2 * step,))
            if chunk is None:
                for i, (low, high) in enumerate(bounds):
                    arrived[i].append(got[:, low:high])
            else:
                arrived[chunk].append(got)

        rest = (driver, vir_energy[None, :], occ_energy[None, :], occ_coupling)
        stages = [[], [], []]
        for c, (low, high) in enumerate(bounds):
            final = c == len(bounds) - 1
            total = totals[c]
            for value in arrived[c]:
                total += value.astype(jnp.float32)
            blocks = total.astype(jnp.float16).reshape(2, pair_n, own_rows, high - low)
            outgoing = [pick(at_pair, [blocks[:, i ^ s] for i in range(pair_n)]) for s in range(pair_n)]
            own = [jnp.where(first_core, o[0], o[1]) for o in outgoing]
            cross = [jnp.where(first_core, o[1], o[0]) for o in outgoing]

            def add(stage, mine_side, step, value):
                stages[stage].append(((mine_side, step, low, high), value.astype(jnp.float32)))

            add(0, True, 0, own[0])
            if final:
                add(1, False, 0, flip(cross[0], "col", (cols_n,), (1,)))
                for step in range(1, pair_n):
                    add(2, True, step, flip(own[step], "pair", (pair_n,), (step,)))
                for step in range(1, pair_n):
                    got = flip(cross[step], ("col", "pair"), (cols_n, pair_n), (1, step))
                    add(2, False, step, got)
            else:
                send = [cross[0]]
                for step in range(1, pair_n):
                    got = flip(outgoing[step], "pair", (pair_n,), (step,))
                    add(0, True, step, jnp.where(first_core, got[0], got[1]))
                    send.append(jnp.where(first_core, got[1], got[0]))
                back = flip(jnp.stack(send), "col", (cols_n,), (1,))
                for step in range(pair_n):
                    add(1, False, step, back[step])

        columns = occ_energy.shape[0]
        begun = None
        for c in range(2):
            kernel = functools.partial(begin_kernel, tuple(p for p, _ in stages[c]), share, begun is not None)
            carried = [] if begun is None else [begun]
            begun = update_call(kernel, own_rows, columns, [], *rest, *(v for _, v in stages[c]), *carried)
        pieces = sum(stages, [])
        last = len(stages[0]) + len(stages[1])
        kernel = functools.partial(finish_kernel, tuple(p for p, _ in pieces), share, last)
        scratch = [pltpu.VMEM((own_rows, columns), jnp.float32)]
        ladders = [v for _, v in pieces]
        return update_call(kernel, own_rows, columns, scratch, *rest, *ladders, begun)

    return jax.shard_map(
        body,
        mesh=mesh,
        in_specs=(
            P("row", "col"),
            P("row", "col"),
            P(("col", "row"), "pair"),
            P(("row", "col", "pair"), None),
            P(("row", "col", "pair")),
            P(),
            P(),
        ),
        out_specs=P(("row", "col", "pair"), None),
        check_vma=False,
    )
```

```python
import functools

import jax
import jax.numpy as jnp
from jax import lax
from jax.experimental.layout import Layout, with_layout_constraint
from jax.experimental import pallas as pl
from jax.experimental.pallas import tpu as pltpu
from jax.sharding import PartitionSpec as P


LANES = 128
SCALE = 8.0


def flip(value, axes, sizes, steps):
    pairs = []
    total = 1
    for size in sizes:
        total *= size
    for source in range(total):
        rest, target, scale = source, 0, 1
        for size, step in zip(reversed(sizes), reversed(steps)):
            target += ((rest % size) ^ step) * scale
            rest //= size
            scale *= size
        pairs.append((source, target))
    return lax.ppermute(value, axes, pairs)


def tall(row):
    count = row.shape[1]
    diagonal = lax.broadcasted_iota(jnp.int32, (count, count), 0) == lax.broadcasted_iota(jnp.int32, (count, count), 1)
    return jnp.sum(jnp.where(diagonal, row[...], 0.0), axis=1, keepdims=True)


def terms(piece, share, ladder, driver, vir, occ):
    mine, step, low, high = piece
    core, pair = lax.axis_index("col") & 1, lax.axis_index("pair")
    part = 2 * (pair ^ step) + (core if mine else 1 - core)
    span = pl.ds(pl.multiple_of(part * share + low, LANES), high - low)
    residual = driver[:, span].astype(jnp.float32) + ladder[...] * (1 / SCALE)
    return span, residual, vir - occ[:, span]


def couple(total, pieces, share, ladders, driver, vir, occ, coupling):
    for piece, ladder in zip(pieces, ladders):
        span, residual, denom = terms(piece, share, ladder, driver, vir, occ)
        scaled = (residual / denom).astype(jnp.bfloat16)
        product = jnp.dot(scaled, coupling[span, :], preferred_element_type=jnp.float32)
        total = product if total is None else total + product
    return total


def begin_kernel(pieces, share, carried, driver, vir, occ, coupling, *refs):
    ladders, out = refs[: len(pieces)], refs[-1]
    total = refs[len(pieces)][...] if carried else None
    out[...] = couple(total, pieces, share, ladders, driver, tall(vir), occ, coupling)


def finish_kernel(pieces, share, last, driver, vir, occ, coupling, *refs):
    ladders, begun, out, coupled = refs[: len(pieces)], *refs[len(pieces) :]
    column = tall(vir)
    coupled[...] = couple(begun[...], pieces[last:], share, ladders[last:], driver, column, occ, coupling)
    for piece, ladder in zip(pieces, ladders):
        span, residual, denom = terms(piece, share, ladder, driver, column, occ)
        out[:, span] = -(residual - coupled[:, span]) / denom


def update_call(kernel, rows, columns, scratch, *args):
    return pl.pallas_call(
        kernel,
        out_shape=jax.ShapeDtypeStruct((rows, columns), jnp.float32),
        scratch_shapes=scratch,
        compiler_params=pltpu.CompilerParams(vmem_limit_bytes=16 * 2**20),
    )(*args)


def fetch_kernel(share, bounds, whole, *refs):
    count = 2 * len(bounds)
    extra = (len(refs) - 1 - count) // 2
    others, outs, sems = refs[:extra], refs[extra:-1], refs[-1]
    core = lax.axis_index("col") & 1
    sources = []
    for low, high in bounds:
        for side in (core, 1 - core):
            start = pl.multiple_of(side * share + low, LANES)
            sources.append(whole.at[:, pl.ds(start, high - low)])
    sources += others
    copies = [pltpu.make_async_copy(source, out, sems.at[i]) for i, (source, out) in enumerate(zip(sources, outs))]
    for copy in copies:
        copy.start()
    for copy in copies:
        copy.wait()


def fetch(value, bounds, *others):
    rows, columns = value.shape
    shapes = [pltpu.VMEM((rows, high - low), value.dtype) for low, high in bounds for _ in range(2)]
    shapes += [pltpu.VMEM(o.shape, o.dtype) for o in others]
    outs = pl.pallas_call(
        functools.partial(fetch_kernel, columns // 2, bounds),
        out_shape=shapes,
        in_specs=[pl.BlockSpec(memory_space=pltpu.HBM)] * (1 + len(others)),
        out_specs=[pl.BlockSpec(memory_space=pltpu.VMEM)] * len(shapes),
        scratch_shapes=[pltpu.SemaphoreType.DMA((len(shapes),))],
        compiler_params=pltpu.CompilerParams(vmem_limit_bytes=4 * 2**20),
        name="fetch",
    )(*[pltpu.with_memory_space_constraint(v, pltpu.HBM) for v in (value, *others)])
    count = 2 * len(bounds)
    return outs[0:count:2], outs[1:count:2], *outs[count:]


def pick(at, options):
    chosen = options[0]
    for here, option in zip(at[1:], options[1:]):
        chosen = jnp.where(here, option, chosen)
    return chosen


FIRST = 2
EARLY = "21"
REST = ((3, 0), (2, 1), (3, 1), (1, 1))


def chunk_bounds(share):
    first = FIRST * LANES
    return [(0, first), (first, share)] if first < share else [(0, share)]


def sends(chips, chunks):
    if chips == 4 and chunks == 2:
        return [(int(e), 0) for e in EARLY] + list(REST)
    steps = sorted(range(1, chips), key=lambda s: (s != chips // 2, s))
    return [(s, None) for s in steps]


def solution(mesh):
    rows_n, cols_n, pair_n = mesh.shape["row"], mesh.shape["col"], mesh.shape["pair"]
    chips = cols_n // 2

    def body(integrals, kept_tiles, amplitudes, driver, vir_energy, occ_energy, occ_coupling):
        row, col, pair = (lax.axis_index(a) for a in ("row", "col", "pair"))
        core, chip = col & 1, col >> 1
        depth, width = amplitudes.shape
        own_rows = driver.shape[0]
        share = width // 2
        bounds = chunk_bounds(share)

        first_core = core == 0
        at_pair = [pair == i for i in range(pair_n)]
        mine, others, kept_tiles = fetch(amplitudes, bounds, kept_tiles)
        mine, others, first_core, at_pair = lax.optimization_barrier((list(mine), list(others), first_core, at_pair))
        far, near = [], []
        for a, b in zip(mine, others):
            blocks = []
            for step in range(1, rows_n):
                blocks.append(flip(a, ("row", "col"), (rows_n, cols_n), (step, 0)))
                blocks.append(flip(b, ("row", "col"), (rows_n, cols_n), (step, 1)))
            far.append(blocks)
        tiles_2 = flip(kept_tiles, "col", (cols_n,), (1,))
        integrals_2 = flip(integrals, "col", (cols_n,), (1,))
        for b in others:
            near.append(flip(b, "col", (cols_n,), (1,)))

        bra, tile = integrals.shape[0], integrals.shape[0] // kept_tiles.shape[0]
        group = bra // chips

        def screened(values, tiles):
            keep = jnp.repeat(tiles.astype(jnp.bfloat16) * SCALE, tile, axis=1)
            values = values * jnp.repeat(keep, tile, axis=0)
            values = jnp.concatenate(
                [lax.dynamic_slice_in_dim(values, (chip ^ o) * group, group, 0) for o in range(chips)], 0
            )
            return [lax.dynamic_slice_in_dim(values, (row ^ s) * depth, depth, 1) for s in range(rows_n)]

        first, second = screened(integrals, kept_tiles), screened(integrals_2, tiles_2)
        left = [m for pairing in zip(first, second) for m in pairing]

        def dot(a, b):
            return with_layout_constraint(jnp.dot(a, b, preferred_element_type=jnp.float32), Layout((0, 1)))

        near_left, far_left = jnp.concatenate(left[:2], 1), jnp.concatenate(left[2:], 1)
        early = []
        for a, b in zip(mine, near):
            early.append(dot(near_left, jnp.concatenate([a, b], 0)))
        early, far[0] = lax.optimization_barrier((early, far[0]))
        parts, halved = [], []
        for i, blocks in enumerate(far):
            late = dot(far_left, jnp.concatenate(blocks, 0))
            parts.append(early[i] + late)
            halved.append(parts[-1].astype(jnp.float16))

        def rows_for(value, step):
            return value[step * group : (step + 1) * group]

        totals = [rows_for(p, 0) for p in parts]
        arrived = [[] for _ in parts]
        for step, chunk in sends(chips, len(bounds)):
            if chunk is None:
                sent = jnp.concatenate([rows_for(h, step) for h in halved], 1)
            else:
                sent = rows_for(halved[chunk], step)
            got = flip(sent, "col", (cols_n,), (2 * step,))
            if chunk is None:
                for i, (low, high) in enumerate(bounds):
                    arrived[i].append(got[:, low:high])
            else:
                arrived[chunk].append(got)

        rest = (driver, vir_energy[None, :], occ_energy[None, :], occ_coupling)
        stages = [[], [], []]
        for c, (low, high) in enumerate(bounds):
            final = c == len(bounds) - 1
            total = totals[c]
            for value in arrived[c]:
                total += value.astype(jnp.float32)
            blocks = total.astype(jnp.float16).reshape(2, pair_n, own_rows, high - low)
            outgoing = [pick(at_pair, [blocks[:, i ^ s] for i in range(pair_n)]) for s in range(pair_n)]
            own = [jnp.where(first_core, o[0], o[1]) for o in outgoing]
            cross = [jnp.where(first_core, o[1], o[0]) for o in outgoing]

            def add(stage, mine_side, step, value):
                stages[stage].append(((mine_side, step, low, high), value.astype(jnp.float32)))

            add(0, True, 0, own[0])
            if final:
                add(1, False, 0, flip(cross[0], "col", (cols_n,), (1,)))
                for step in range(1, pair_n):
                    add(2, True, step, flip(own[step], "pair", (pair_n,), (step,)))
                for step in range(1, pair_n):
                    got = flip(cross[step], ("col", "pair"), (cols_n, pair_n), (1, step))
                    add(2, False, step, got)
            else:
                send = [cross[0]]
                for step in range(1, pair_n):
                    got = flip(outgoing[step], "pair", (pair_n,), (step,))
                    add(0, True, step, jnp.where(first_core, got[0], got[1]))
                    send.append(jnp.where(first_core, got[1], got[0]))
                back = flip(jnp.stack(send), "col", (cols_n,), (1,))
                for step in range(pair_n):
                    add(1, False, step, back[step])

        columns = occ_energy.shape[0]
        begun = None
        for c in range(2):
            kernel = functools.partial(begin_kernel, tuple(p for p, _ in stages[c]), share, begun is not None)
            carried = [] if begun is None else [begun]
            begun = update_call(kernel, own_rows, columns, [], *rest, *(v for _, v in stages[c]), *carried)
        pieces = sum(stages, [])
        last = len(stages[0]) + len(stages[1])
        kernel = functools.partial(finish_kernel, tuple(p for p, _ in pieces), share, last)
        scratch = [pltpu.VMEM((own_rows, columns), jnp.float32)]
        ladders = [v for _, v in pieces]
        return update_call(kernel, own_rows, columns, scratch, *rest, *ladders, begun)

    return jax.shard_map(
        body,
        mesh=mesh,
        in_specs=(
            P("row", "col"),
            P("row", "col"),
            P(("col", "row"), "pair"),
            P(("row", "col", "pair"), None),
            P(("row", "col", "pair")),
            P(),
            P(),
        ),
        out_specs=P(("row", "col", "pair"), None),
        check_vma=False,
    )
```
